32 devices in a mesh: depth: 4 (over z), tile: 8 (over y, x, core).
Axes of the slice: x: 2, y: 2, z: 4, core: 2. Of those that a mesh axis runs over, the one named last changes fastest.
Arguments:
- patches: float32 [512, 64, 1024], P('tile', 'depth'), may hold values from 0.1 to 10
- patch_slot: int32 [512], P('tile'), may hold values from 0 to 511, as said below
Outputs:
- image: float32 [8, 64, 4, 1024], P('tile', 'depth')
The draws below stay inside these ranges and needn't reach their ends.
Inputs may be any that keep to these rules, and one draw needn't show every extreme that they name: patch_slot is a permutation of the slots. Device s of tile (patches s * 64 to (s + 1) * 64 - 1) sends to owner t a number that depends only on (t - s) mod 8: one such difference, drawn from the seed, carries 24 patches, two carry none, the others 64 // 8. Every owner receives 64 patches.
All inputs are finite; a program needn't handle non-finite values.
Results may differ from the reference program's by a relative error of at most 0.00002.
Values sent between devices are 32-bit elements; how exact they have to be, the bound alone decides.
A program may use at most 128 MiB of HBM per device.

```python
import math
import jax
import jax.numpy as jnp
from jax import lax

PIX = 1024
PATCH_DEV = 64
NZ = 64
PATCHES = 512
N_TILE = 8


def draw_patch_slot(key, part):
    tiles = N_TILE
    per = PATCH_DEV
    share = per // tiles
    first_key, second_key, third_key = jax.random.split(key, 3)
    order = jax.random.permutation(first_key, tiles)
    weights = jnp.full((tiles,), share, jnp.int32)
    weights = weights.at[order[0]].set(3 * share).at[order[1]].set(0).at[order[2]].set(0)
    sources = jnp.arange(tiles, dtype=jnp.int32)[:, None]
    targets = jnp.arange(tiles, dtype=jnp.int32)[None, :]
    counts = weights[(targets - sources) % tiles]
    base = jnp.cumsum(counts, axis=0) - counts
    running = jnp.cumsum(weights)
    places = jnp.arange(per, dtype=jnp.int32)
    shifts = jnp.sum((places[:, None] >= running[None, :]).astype(jnp.int32), axis=1)
    within = places - (running - weights)[shifts]
    owners = (sources + shifts[None, :]) % tiles
    ranking = jnp.take_along_axis(base, owners, axis=1) + within[None, :]
    shuffles = jax.vmap(lambda sub: jax.random.permutation(sub, per))(jax.random.split(second_key, tiles))
    offsets = shuffles[owners, ranking]
    slots = owners * per + offsets
    reorder = jax.vmap(lambda sub: jax.random.permutation(sub, per))(jax.random.split(third_key, tiles))
    return jnp.take_along_axis(slots, reorder, axis=1).reshape(tiles * per).astype(jnp.int32)


def block_scale(stream_key, shape, cuts, least, largest):
    gain, own = 1.0, jax.random.fold_in(stream_key, 6)
    for axis_at, shards_of in cuts:
        heights = jnp.exp(jax.random.uniform(jax.random.fold_in(own, axis_at), (shards_of,), jnp.float32, least / len(cuts), largest / len(cuts)))
        gain = gain * jnp.repeat(heights, shape[axis_at] // shards_of).reshape([-1 if axis == axis_at else 1 for axis in range(len(shape))])
    return gain


def setup_inputs(seed: int = 0) -> dict:
    key_list = jax.random.split(jax.random.key(seed), 3)
    patches = jnp.clip(jnp.exp(math.log(10.0) - 4.6051702 * jax.random.uniform(key_list[0], (PATCHES, NZ, PIX), jnp.float32) ** block_scale(key_list[0], (PATCHES, NZ, PIX), ((0, 8), (1, 4)), -0.2, 0.2)), 0.1, 10.0)
    patch_slot = draw_patch_slot(jax.random.fold_in(key_list[2], 71), 0)
    return {"patches": patches, "patch_slot": patch_slot}


def shade_rays(padded, depth_total):
    level = padded[:, 1:-1]
    slope = (padded[:, 2:] - padded[:, :-2]) * 0.5
    sigma = 0.6 * jnp.exp(-(level - 0.5) ** 2) + 0.4 * jnp.exp(-2.0 * (level + 1.0) ** 2) + 0.3 * slope * slope
    optical = sigma * (2.0 / depth_total)
    depth_sum = jnp.cumsum(optical, axis=1)
    weight = jnp.exp(-(depth_sum - optical)) * (1.0 - jnp.exp(-optical))
    lighting = weight / (1.0 + slope * slope)
    red = jnp.sum(lighting * jax.nn.sigmoid(2.0 * level), axis=1)
    green = jnp.sum(lighting * jnp.exp(-level * level), axis=1)
    blue = jnp.sum(lighting * jax.nn.sigmoid(-2.0 * level), axis=1)
    remain = jnp.exp(-depth_sum[:, -1])
    return jnp.stack([red, green, blue, remain], axis=1)


def render_group(density):
    level = jnp.log(density)
    padded = jnp.pad(level, ((0, 0), (1, 1), (0, 0)))
    return shade_rays(padded, NZ)


def reference(patches, patch_slot):
    groups = patches.reshape(N_TILE, PATCH_DEV, NZ, PIX)
    rendered = lax.map(render_group, groups).reshape(PATCHES, 4, PIX)
    placed = jnp.zeros_like(rendered).at[patch_slot].set(rendered)
    color = placed[:, :3]
    alpha = 1.0 - placed[:, 3:]
    return jnp.concatenate([color, alpha], axis=1).reshape(N_TILE, PATCH_DEV, 4, PIX)
```

```python
import functools
import math

import jax
import jax.numpy as jnp
from jax import lax
from jax.experimental import pallas as pl
from jax.experimental.pallas import tpu as pltpu
from jax.sharding import PartitionSpec as P

BLOCK = 8
GROUPS = 2
LANES = 128
LABEL_ROWS = 8


def halos(patches):
    count = lax.axis_size("depth")
    forward = [(i, i + 1) for i in range(count - 1)]
    backward = [(target, source) for source, target in forward]
    low = lax.ppermute(jnp.log(patches[:, -1]), "depth", forward)
    high = lax.ppermute(jnp.log(patches[:, 0]), "depth", backward)
    return low, high


def shade_kernel(cells, scale, x_ref, low_ref, high_ref, out_ref):
    first = 0.6 * math.exp(-0.25) * scale
    second = 0.4 * math.exp(-2.0) * scale
    third = 0.3 * scale
    rows = GROUPS * BLOCK

    def plane(step, cell):
        base = step * (rows * cells) + cell
        return jnp.stack(
            [
                x_ref[pl.ds(base + group * BLOCK * cells, BLOCK, stride=cells), :]
                for group in range(GROUPS)
            ]
        )

    def patch_rows(step):
        return pl.ds(pl.multiple_of(step * rows, rows), rows)

    @pl.loop(0, low_ref.shape[0] // rows)
    def _(step):
        shape = (GROUPS, BLOCK, low_ref.shape[1])
        before = low_ref[patch_rows(step), :].reshape(shape)
        x = plane(step, 0)
        level = jnp.log(x)
        clear = jnp.ones_like(x)
        red = green = blue = jnp.zeros_like(x)
        for cell in range(cells):
            if cell + 1 < cells:
                x_after = plane(step, cell + 1)
                after = jnp.log(x_after)
            else:
                x_after, after = None, high_ref[patch_rows(step), :].reshape(shape)
            slope = (after - before) * 0.5
            slope2 = slope * slope
            square = x * x
            bell = jnp.exp(-level * level)
            wide = 1.0 + square
            below = wide * (1.0 + slope2)
            inverse = 1.0 / (square * below)
            ratio = bell * (inverse * below)
            optical = first * (bell * x) + second * (ratio * ratio) + third * slope2
            pass_on = jnp.exp(-optical)
            light = clear * (1.0 - pass_on) * (inverse * square)
            clear = clear * pass_on
            blue = blue + light
            red = red + light * square
            green = green + light * (bell * wide)
            before, level, x = level, after, x_after
        for c, value in enumerate((red, green, blue, clear)):
            out_ref[0, c, patch_rows(step), :] = value.reshape(rows, shape[2])


def shade(patches, low, high, quarters):
    per, cells, rays = patches.shape
    scale = 2.0 / (cells * quarters)
    width = rays // quarters
    halves = width // LANES
    return pl.pallas_call(
        functools.partial(shade_kernel, cells, scale),
        grid=(rays // LANES,),
        out_shape=jax.ShapeDtypeStruct((quarters, 4, per, width), jnp.float32),
        in_specs=[
            pl.BlockSpec((per * cells, LANES), lambda i: (0, i)),
            pl.BlockSpec((per, LANES), lambda i: (0, i)),
            pl.BlockSpec((per, LANES), lambda i: (0, i)),
        ],
        out_specs=pl.BlockSpec(
            (1, 4, per, LANES), lambda i: (i // halves, 0, 0, i % halves)
        ),
        name="shade",
    )(patches.reshape(per * cells, rays), low, high)


def composite(layers_ref, part):
    quarters = layers_ref.shape[0]
    color = [layers_ref[0, c] for c in range(3)]
    clear = layers_ref[0, 3]
    for depth in range(1, quarters):
        for c in range(3):
            color[c] = color[c] + clear * layers_ref[depth, c]
        clear = clear * layers_ref[depth, 3]
    return color + [clear]


def pack_kernel(tiles, slots, layers_ref, row_ref, col_ref, out_ref):
    per = row_ref.shape[1]
    width = out_ref.shape[2]
    row, col = row_ref[...], col_ref[...]
    shift = per.bit_length() - 1
    dest_row, dest_col = row >> shift, col >> shift
    same = (dest_col == dest_row).astype(jnp.float32)
    down = lax.broadcasted_iota(jnp.int32, (per, per), 0)
    across = lax.broadcasted_iota(jnp.int32, (per, per), 1)
    rank_row = jnp.sum(jnp.where(down < across, same, 0.0), axis=0, keepdims=True)
    rank_col = jnp.sum(jnp.where(across < down, same, 0.0), axis=1, keepdims=True)
    target_row = dest_row * slots + rank_row.astype(jnp.int32)
    target_col = dest_col * slots + rank_col.astype(jnp.int32)
    offset = (col & (per - 1)).astype(jnp.float32) + 1.0
    choice = (
        lax.broadcasted_iota(jnp.int32, (tiles * slots, per), 0) == target_row
    ).astype(jnp.float32)
    values = composite(layers_ref, None)
    for c in range(4):
        packed = jnp.dot(
            choice,
            values[c],
            precision=lax.Precision.HIGHEST,
            preferred_element_type=jnp.float32,
        )
        out_ref[:, c * slots : (c + 1) * slots, :] = packed.reshape(tiles, slots, width)
    lane = lax.broadcasted_iota(jnp.int32, (per, width), 1)
    for tile in range(tiles):
        hit = (target_col == tile * slots + lane) & (lane < slots)
        mark = jnp.sum(jnp.where(hit, offset, 0.0), axis=0, keepdims=True) - 1.0
        out_ref[tile, 4 * slots :, :] = jnp.broadcast_to(mark, (LABEL_ROWS, width))


def pack(layers, patch_slot, tiles, slots):
    per = patch_slot.shape[0]
    width = layers.shape[3]
    return pl.pallas_call(
        functools.partial(pack_kernel, tiles, slots),
        out_shape=jax.ShapeDtypeStruct((tiles, 4 * slots + LABEL_ROWS, width), jnp.float32),
        name="pack",
    )(layers, patch_slot.reshape(1, per), patch_slot.reshape(per, 1))


def place_kernel(slots, got_ref, out_ref):
    tiles, width = got_ref.shape[0], got_ref.shape[2]
    quarters, _, share, _ = out_ref.shape
    per = quarters * share
    place = lax.broadcasted_iota(jnp.int32, (per, slots), 0)
    totals = [jnp.zeros((per, width), jnp.float32) for _ in range(4)]
    for tile in range(tiles):
        mark = got_ref[tile, 4 * slots : 4 * slots + 1, :][:, :slots].astype(jnp.int32)
        choice = (place == mark).astype(jnp.float32)
        for c in range(4):
            totals[c] = totals[c] + jnp.dot(
                choice,
                got_ref[tile, c * slots : (c + 1) * slots, :],
                precision=lax.Precision.HIGHEST,
                preferred_element_type=jnp.float32,
            )
    totals[3] = 1.0 - totals[3]
    for c in range(4):
        out_ref[:, c] = totals[c].reshape(quarters, share, width)


def place(got, per, quarters, slots):
    width = got.shape[2]
    return pl.pallas_call(
        functools.partial(place_kernel, slots),
        out_shape=jax.ShapeDtypeStruct((quarters, 4, per // quarters, width), jnp.float32),
        name="place",
    )(got)


def swap(array, axis):
    return lax.all_to_all(array, axis, split_axis=0, concat_axis=0, tiled=True)


def local(patches, patch_slot):
    per, _, rays = patches.shape
    tiles = lax.axis_size("tile")
    quarters = lax.axis_size("depth")
    slots = -(-(3 * per // tiles) // 8) * 8
    low, high = halos(patches)
    layers = swap(shade(patches, low, high, quarters), "depth")
    got = swap(pack(layers, patch_slot, tiles, slots), "tile")
    final = swap(place(got, per, quarters, slots), "depth")
    return final.transpose(2, 1, 0, 3).reshape(1, per // quarters, 4, rays)


def solution(mesh):
    return jax.shard_map(
        local,
        mesh=mesh,
        in_specs=(P("tile", "depth", None), P("tile")),
        out_specs=P("tile", "depth", None, None),
        check_vma=False,
    )
```

```python
import functools
import math

import jax
import jax.numpy as jnp
from jax import lax
from jax.experimental import pallas as pl
from jax.experimental.pallas import tpu as pltpu
from jax.sharding import PartitionSpec as P

BLOCK = 8
GROUPS = 2
LANES = 128
MESH = pl.DeviceIdType.MESH
LABEL_ROWS = 8


def ray_cell(scale, state, x, before, level, after):
    red, green, blue, clear = state
    slope = (after - before) * 0.5
    slope2 = slope * slope
    square = x * x
    bell = jnp.exp(-level * level)
    wide = 1.0 + square
    below = wide * (1.0 + slope2)
    inverse = 1.0 / (square * below)
    ratio = bell * (inverse * below)
    optical = (
        (0.6 * math.exp(-0.25) * scale) * (bell * x)
        + (0.4 * math.exp(-2.0) * scale) * (ratio * ratio)
        + (0.3 * scale) * slope2
    )
    pass_on = jnp.exp(-optical)
    light = clear * (1.0 - pass_on) * (inverse * square)
    return (
        red + light * square,
        green + light * (bell * wide),
        blue + light,
        clear * pass_on,
    )


def over(front, back):
    clear = front[3]
    return tuple(front[c] + clear * back[c] for c in range(3)) + (clear * back[3],)


def greet(peers):
    barrier = pltpu.get_barrier_semaphore()
    for peer in peers:
        pl.semaphore_signal(barrier, inc=1, device_id=peer, device_id_type=MESH)
    pl.semaphore_wait(barrier, len(peers))


def front_kernel(
    cells, quarters, scale, x_hbm, out_ref,
    x_ref, edge, halo, part, got, load_sem, edge_send, edge_recv, send_sem, recv_sem,
):
    me = lax.axis_index("depth")
    _, per, width = out_ref.shape
    halves = width // LANES
    chunks = quarters * halves
    rows = GROUPS * BLOCK
    shape = (GROUPS, BLOCK, LANES)
    loads = [
        pltpu.make_async_copy(
            x_hbm.at[:, pl.ds(j * LANES, LANES)], x_ref.at[j], load_sem.at[j]
        )
        for j in range(chunks)
    ]
    for load in loads:
        load.start()
    greet([{"depth": lax.rem(me + k, quarters)} for k in range(1, quarters)])

    def plane(chunk, step, cell):
        base = step * (rows * cells) + cell
        return jnp.stack(
            [
                x_ref[chunk, pl.ds(base + g * BLOCK * cells, BLOCK, stride=cells), :]
                for g in range(GROUPS)
            ]
        )

    def patch_rows(step):
        return pl.ds(pl.multiple_of(step * rows, rows), rows)

    for j in range(chunks):
        loads[j].wait()

        @pl.loop(0, per // rows)
        def _(step):
            for side, cell in enumerate((0, cells - 1)):
                value = jnp.log(plane(j, step, cell)).reshape(rows, LANES)
                edge[side, patch_rows(step), pl.ds(j * LANES, LANES)] = value

    def edge_copy(side, source, peer):
        return pltpu.make_async_remote_copy(
            src_ref=edge.at[source],
            dst_ref=halo.at[side],
            send_sem=edge_send.at[side],
            recv_sem=edge_recv.at[side],
            device_id={"depth": peer},
            device_id_type=MESH,
        )

    up = edge_copy(0, 1, lax.rem(me + 1, quarters))
    down = edge_copy(1, 0, lax.rem(me + quarters - 1, quarters))

    @pl.when(me < quarters - 1)
    def _():
        up.start()

    @pl.when(me > 0)
    def _():
        down.start()

    @pl.when(me == 0)
    def _():
        halo[0] = jnp.zeros_like(halo[0])

    @pl.when(me == quarters - 1)
    def _():
        halo[1] = jnp.zeros_like(halo[1])

    ones = functools.partial(jnp.ones, shape, jnp.float32)
    zeros = functools.partial(jnp.zeros, shape, jnp.float32)

    @pl.loop(0, chunks)
    def _(chunk):
        quarter = chunk // halves
        lanes = pl.ds(pl.multiple_of((chunk % halves) * LANES, LANES), LANES)

        @pl.loop(0, per // rows)
        def _(step):
            before = jnp.log(plane(chunk, step, 0))
            x = plane(chunk, step, 1)
            level = jnp.log(x)
            state = (zeros(), zeros(), zeros(), ones())
            for cell in range(1, cells - 1):
                x_after = plane(chunk, step, cell + 1)
                after = jnp.log(x_after)
                state = ray_cell(scale, state, x, before, level, after)
                before, level, x = level, after, x_after
            for c in range(4):
                part[quarter, c, patch_rows(step), lanes] = state[c].reshape(rows, LANES)

    @pl.when(me > 0)
    def _():
        up.wait_recv()

    @pl.when(me < quarters - 1)
    def _():
        down.wait_recv()

    def piece(quarter, source, peer):
        return pltpu.make_async_remote_copy(
            src_ref=part.at[quarter],
            dst_ref=got.at[source],
            send_sem=send_sem.at[peer],
            recv_sem=recv_sem.at[source],
            device_id={"depth": peer},
            device_id_type=MESH,
        )

    def finish(quarter, store):
        for half in range(halves):
            chunk = quarter * halves + half
            lanes = pl.ds(half * LANES, LANES)
            wide = pl.ds(pl.multiple_of(chunk * LANES, LANES), LANES)

            @pl.loop(0, per // rows)
            def _(step):
                start = (zeros(), zeros(), zeros(), ones())
                x = plane(chunk, step, 0)
                first = ray_cell(
                    scale, start, x,
                    halo[0, patch_rows(step), wide].reshape(shape),
                    jnp.log(x),
                    jnp.log(plane(chunk, step, 1)),
                )
                x = plane(chunk, step, cells - 1)
                last = ray_cell(
                    scale, start, x,
                    jnp.log(plane(chunk, step, cells - 2)),
                    jnp.log(x),
                    halo[1, patch_rows(step), wide].reshape(shape),
                )
                inner = tuple(
                    part[quarter, c, patch_rows(step), lanes].reshape(shape)
                    for c in range(4)
                )
                total = over(over(first, inner), last)
                for c in range(4):
                    store(c, patch_rows(step), lanes, total[c].reshape(rows, LANES))

    for k in range(1, quarters):
        target = lax.rem(me + k, quarters)

        def keep(c, at, lanes, value, target=target):
            part[target, c, at, lanes] = value

        finish(target, keep)
        piece(target, me, target).start()

    def own(c, at, lanes, value):
        got[me, c, at, lanes] = value

    finish(me, own)
    for k in range(1, quarters):
        source = lax.rem(me + k, quarters)
        piece(me, source, source).wait_recv()
    total = tuple(got[0, c] for c in range(4))
    for depth in range(1, quarters):
        total = over(total, tuple(got[depth, c] for c in range(4)))
    for c in range(4):
        out_ref[c] = total[c]
    for k in range(1, quarters):
        target = lax.rem(me + k, quarters)
        piece(target, me, target).wait_send()

    @pl.when(me < quarters - 1)
    def _():
        up.wait_send()

    @pl.when(me > 0)
    def _():
        down.wait_send()


def front(patches, quarters):
    per, cells, rays = patches.shape
    width = rays // quarters
    chunks = rays // LANES
    dma = pltpu.SemaphoreType.DMA
    return pl.pallas_call(
        functools.partial(front_kernel, cells, quarters, 2.0 / (cells * quarters)),
        out_shape=jax.ShapeDtypeStruct((4, per, width), jnp.float32),
        in_specs=[pl.BlockSpec(memory_space=pl.ANY)],
        out_specs=pl.BlockSpec(memory_space=pltpu.VMEM),
        scratch_shapes=[
            pltpu.VMEM((chunks, per * cells, LANES), jnp.float32),
            pltpu.VMEM((2, per, rays), jnp.float32),
            pltpu.VMEM((2, per, rays), jnp.float32),
            pltpu.VMEM((quarters, 4, per, width), jnp.float32),
            pltpu.VMEM((quarters, 4, per, width), jnp.float32),
            dma((chunks,)),
            dma((2,)),
            dma((2,)),
            dma((quarters,)),
            dma((quarters,)),
        ],
        compiler_params=pltpu.CompilerParams(collective_id=0, has_side_effects=True),
        name="front",
    )(patches.reshape(per * cells, rays))


def pack(tiles, slots, values_ref, row_ref, col_ref, out_ref):
    per = row_ref.shape[1]
    width = out_ref.shape[2]
    row, col = row_ref[...], col_ref[...]
    shift = per.bit_length() - 1
    dest_row, dest_col = row >> shift, col >> shift
    same = (dest_col == dest_row).astype(jnp.float32)
    down = lax.broadcasted_iota(jnp.int32, (per, per), 0)
    across = lax.broadcasted_iota(jnp.int32, (per, per), 1)
    rank_row = jnp.sum(jnp.where(down < across, same, 0.0), axis=0, keepdims=True)
    rank_col = jnp.sum(jnp.where(across < down, same, 0.0), axis=1, keepdims=True)
    target_row = dest_row * slots + rank_row.astype(jnp.int32)
    target_col = dest_col * slots + rank_col.astype(jnp.int32)
    offset = (col & (per - 1)).astype(jnp.float32) + 1.0
    choice = (
        lax.broadcasted_iota(jnp.int32, (tiles * slots, per), 0) == target_row
    ).astype(jnp.float32)
    for c in range(4):
        packed = jnp.dot(
            choice,
            values_ref[c],
            precision=lax.Precision.HIGHEST,
            preferred_element_type=jnp.float32,
        )
        out_ref[:, c * slots : (c + 1) * slots, :] = packed.reshape(tiles, slots, width)
    lane = lax.broadcasted_iota(jnp.int32, (per, width), 1)
    for tile in range(tiles):
        hit = (target_col == tile * slots + lane) & (lane < slots)
        mark = jnp.sum(jnp.where(hit, offset, 0.0), axis=0, keepdims=True) - 1.0
        out_ref[tile, 4 * slots :, :] = jnp.broadcast_to(mark, (LABEL_ROWS, width))


def place(slots, got_ref, out_ref):
    tiles, width = got_ref.shape[0], got_ref.shape[2]
    quarters, _, share, _ = out_ref.shape
    per = quarters * share
    at = lax.broadcasted_iota(jnp.int32, (per, slots), 0)
    totals = [jnp.zeros((per, width), jnp.float32) for _ in range(4)]
    for tile in range(tiles):
        mark = got_ref[tile, 4 * slots : 4 * slots + 1, :][:, :slots].astype(jnp.int32)
        choice = (at == mark).astype(jnp.float32)
        for c in range(4):
            totals[c] = totals[c] + jnp.dot(
                choice,
                got_ref[tile, c * slots : (c + 1) * slots, :],
                precision=lax.Precision.HIGHEST,
                preferred_element_type=jnp.float32,
            )
    totals[3] = 1.0 - totals[3]
    for c in range(4):
        out_ref[:, c] = totals[c].reshape(quarters, share, width)


def exchange(axis, count, source_ref, got_ref, send_sem, recv_sem):
    me = lax.axis_index(axis)

    def copy(piece, source, peer):
        return pltpu.make_async_remote_copy(
            src_ref=source_ref.at[piece],
            dst_ref=got_ref.at[source],
            send_sem=send_sem.at[peer],
            recv_sem=recv_sem.at[source],
            device_id={axis: peer},
            device_id_type=MESH,
        )

    peers = [lax.rem(me + k, count) for k in range(1, count)]
    for peer in peers:
        copy(peer, me, peer).start()
    got_ref[me] = source_ref[me]
    for peer in peers:
        copy(me, peer, peer).wait_recv()
    for peer in peers:
        copy(peer, me, peer).wait_send()


def back_kernel(
    tiles, quarters, slots, values_ref, row_ref, col_ref, out_ref,
    packed, got, placed, landed, tile_send, tile_recv, depth_send, depth_recv,
):
    peers = [
        {axis: lax.rem(lax.axis_index(axis) + k, count)}
        for axis, count in (("tile", tiles), ("depth", quarters))
        for k in range(1, count)
    ]
    greet(peers)
    pack(tiles, slots, values_ref, row_ref, col_ref, packed)
    exchange("tile", tiles, packed, got, tile_send, tile_recv)
    place(slots, got, placed)
    exchange("depth", quarters, placed, landed, depth_send, depth_recv)
    out_ref[...] = landed[...]


def back(values, patch_slot, tiles, quarters, slots):
    _, per, width = values.shape
    dma = pltpu.SemaphoreType.DMA
    result = (quarters, 4, per // quarters, width)
    block = (tiles, 4 * slots + LABEL_ROWS, width)
    return pl.pallas_call(
        functools.partial(back_kernel, tiles, quarters, slots),
        out_shape=jax.ShapeDtypeStruct(result, jnp.float32),
        in_specs=[pl.BlockSpec(memory_space=pltpu.VMEM)] * 3,
        out_specs=pl.BlockSpec(memory_space=pltpu.VMEM),
        scratch_shapes=[
            pltpu.VMEM(block, jnp.float32),
            pltpu.VMEM(block, jnp.float32),
            pltpu.VMEM(result, jnp.float32),
            pltpu.VMEM(result, jnp.float32),
            dma((tiles,)),
            dma((tiles,)),
            dma((quarters,)),
            dma((quarters,)),
        ],
        compiler_params=pltpu.CompilerParams(collective_id=1, has_side_effects=True),
        name="back",
    )(values, patch_slot.reshape(1, per), patch_slot.reshape(per, 1))


def local(patches, patch_slot):
    per, _, rays = patches.shape
    tiles = lax.axis_size("tile")
    quarters = lax.axis_size("depth")
    slots = -(-(3 * per // tiles) // 8) * 8
    values = front(patches, quarters)
    final = back(values, patch_slot, tiles, quarters, slots)
    return final.transpose(2, 1, 0, 3).reshape(1, per // quarters, 4, rays)


def solution(mesh):
    return jax.shard_map(
        local,
        mesh=mesh,
        in_specs=(P("tile", "depth", None), P("tile")),
        out_specs=P("tile", "depth", None, None),
        check_vma=False,
    )
```

```python
import functools
import math

import jax
import jax.numpy as jnp
from jax import lax
from jax.experimental import pallas as pl
from jax.experimental.pallas import tpu as pltpu
from jax.sharding import PartitionSpec as P

BLOCK = 8
GROUPS = 2
LANES = 128
MESH = pl.DeviceIdType.MESH
LABEL_ROWS = 8


def ray_cell(scale, state, x, before, level, after):
    red, green, blue, clear = state
    slope = (after - before) * 0.5
    slope2 = slope * slope
    square = x * x
    bell = jnp.exp(-level * level)
    wide = 1.0 + square
    below = wide * (1.0 + slope2)
    inverse = 1.0 / (square * below)
    ratio = bell * (inverse * below)
    optical = (
        (0.6 * math.exp(-0.25) * scale) * (bell * x)
        + (0.4 * math.exp(-2.0) * scale) * (ratio * ratio)
        + (0.3 * scale) * slope2
    )
    pass_on = jnp.exp(-optical)
    light = clear * (1.0 - pass_on) * (inverse * square)
    return (
        red + light * square,
        green + light * (bell * wide),
        blue + light,
        clear * pass_on,
    )


def over(front, back):
    clear = front[3]
    return tuple(front[c] + clear * back[c] for c in range(3)) + (clear * back[3],)


def greet(peers):
    barrier = pltpu.get_barrier_semaphore()
    for peer in peers:
        pl.semaphore_signal(barrier, inc=1, device_id=peer, device_id_type=MESH)
    pl.semaphore_wait(barrier, len(peers))


def front_kernel(
    cells, quarters, scale, x_hbm, out_ref,
    x_ref, edge, halo, part, got, load_sem, edge_send, edge_recv, send_sem, recv_sem,
):
    me = lax.axis_index("depth")
    _, per, width = out_ref.shape
    halves = width // LANES
    chunks = quarters * halves
    rows = GROUPS * BLOCK
    shape = (GROUPS, BLOCK, LANES)
    loads = [
        pltpu.make_async_copy(
            x_hbm.at[:, pl.ds(j * LANES, LANES)], x_ref.at[j], load_sem.at[j]
        )
        for j in range(chunks)
    ]
    for load in loads:
        load.start()
    greet([{"depth": lax.rem(me + k, quarters)} for k in range(1, quarters)])

    def plane(chunk, step, cell):
        base = step * (rows * cells) + cell
        return jnp.stack(
            [
                x_ref[chunk, pl.ds(base + g * BLOCK * cells, BLOCK, stride=cells), :]
                for g in range(GROUPS)
            ]
        )

    def patch_rows(step):
        return pl.ds(pl.multiple_of(step * rows, rows), rows)

    for j in range(chunks):
        loads[j].wait()

        @pl.loop(0, per // rows)
        def _(step):
            for side, cell in enumerate((0, cells - 1)):
                value = jnp.log(plane(j, step, cell)).reshape(rows, LANES)
                edge[side, patch_rows(step), pl.ds(j * LANES, LANES)] = value

    def edge_copy(side, source, peer):
        return pltpu.make_async_remote_copy(
            src_ref=edge.at[source],
            dst_ref=halo.at[side],
            send_sem=edge_send.at[side],
            recv_sem=edge_recv.at[side],
            device_id={"depth": peer},
            device_id_type=MESH,
        )

    up = edge_copy(0, 1, lax.rem(me + 1, quarters))
    down = edge_copy(1, 0, lax.rem(me + quarters - 1, quarters))

    @pl.when(me < quarters - 1)
    def _():
        up.start()

    @pl.when(me > 0)
    def _():
        down.start()

    @pl.when(me == 0)
    def _():
        halo[0] = jnp.zeros_like(halo[0])

    @pl.when(me == quarters - 1)
    def _():
        halo[1] = jnp.zeros_like(halo[1])

    ones = functools.partial(jnp.ones, shape, jnp.float32)
    zeros = functools.partial(jnp.zeros, shape, jnp.float32)

    @pl.loop(0, chunks)
    def _(chunk):
        quarter = chunk // halves
        lanes = pl.ds(pl.multiple_of((chunk % halves) * LANES, LANES), LANES)

        @pl.loop(0, per // rows)
        def _(step):
            before = jnp.log(plane(chunk, step, 0))
            x = plane(chunk, step, 1)
            level = jnp.log(x)
            state = (zeros(), zeros(), zeros(), ones())
            for cell in range(1, cells - 1):
                x_after = plane(chunk, step, cell + 1)
                after = jnp.log(x_after)
                state = ray_cell(scale, state, x, before, level, after)
                before, level, x = level, after, x_after
            for c in range(4):
                part[quarter, c, patch_rows(step), lanes] = state[c].reshape(rows, LANES)

    @pl.when(me > 0)
    def _():
        up.wait_recv()

    @pl.when(me < quarters - 1)
    def _():
        down.wait_recv()

    def hop(side, quarter):
        peer = lax.rem(me + (quarters - 1 if side else 1), quarters)
        return pltpu.make_async_remote_copy(
            src_ref=part.at[quarter],
            dst_ref=got.at[side, quarter],
            send_sem=send_sem.at[side, quarter],
            recv_sem=recv_sem.at[side, quarter],
            device_id={"depth": peer},
            device_id_type=MESH,
        )

    def finish(quarter):
        for half in range(halves):
            chunk = quarter * halves + half
            lanes = pl.ds(half * LANES, LANES)
            wide = pl.ds(pl.multiple_of(chunk * LANES, LANES), LANES)

            @pl.loop(0, per // rows)
            def _(step):
                start = (zeros(), zeros(), zeros(), ones())
                x = plane(chunk, step, 0)
                first = ray_cell(
                    scale, start, x,
                    halo[0, patch_rows(step), wide].reshape(shape),
                    jnp.log(x),
                    jnp.log(plane(chunk, step, 1)),
                )
                x = plane(chunk, step, cells - 1)
                last = ray_cell(
                    scale, start, x,
                    jnp.log(plane(chunk, step, cells - 2)),
                    jnp.log(x),
                    halo[1, patch_rows(step), wide].reshape(shape),
                )
                inner = tuple(
                    part[quarter, c, patch_rows(step), lanes].reshape(shape)
                    for c in range(4)
                )
                total = over(over(first, inner), last)
                for c in range(4):
                    part[quarter, c, patch_rows(step), lanes] = total[c].reshape(rows, LANES)

    last = quarters - 1
    near = (me < quarters // 2).astype(jnp.int32)
    for k in range(quarters):
        quarter = k + near * (last - 2 * k)
        finish(quarter)
        if k < last:
            for side, end in enumerate((0, last)):
                @pl.when(me == end)
                def _():
                    hop(side, last - k if side == 0 else k).start()

    def merge(side, quarter):
        own = tuple(part[quarter, c] for c in range(4))
        come = tuple(got[side, quarter, c] for c in range(4))
        total = over(own, come) if side else over(come, own)
        for c in range(4):
            part[quarter, c] = total[c]

    def turn(side, t):
        rank = last - me if side else me
        quarter = t - rank if side else last - t + rank
        return rank, quarter

    for t in range(1, last):
        for side in (0, 1):
            rank, quarter = turn(side, t)

            @pl.when((rank >= 1) & (rank <= t))
            def _():
                hop(side, quarter).wait_recv()
                merge(side, quarter)
                hop(side, quarter).start()

    for side, end in enumerate((0, last)):
        @pl.when(me != end)
        def _():
            hop(side, me).wait_recv()
            merge(side, me)

    for c in range(4):
        out_ref[c] = part[me, c]
    for t in range(last):
        for side in (0, 1):
            rank, quarter = turn(side, t)

            @pl.when(rank <= t)
            def _():
                hop(side, quarter).wait_send()

    @pl.when(me < quarters - 1)
    def _():
        up.wait_send()

    @pl.when(me > 0)
    def _():
        down.wait_send()


def front(patches, quarters):
    per, cells, rays = patches.shape
    width = rays // quarters
    chunks = rays // LANES
    dma = pltpu.SemaphoreType.DMA
    return pl.pallas_call(
        functools.partial(front_kernel, cells, quarters, 2.0 / (cells * quarters)),
        out_shape=jax.ShapeDtypeStruct((4, per, width), jnp.float32),
        in_specs=[pl.BlockSpec(memory_space=pl.ANY)],
        out_specs=pl.BlockSpec(memory_space=pltpu.VMEM),
        scratch_shapes=[
            pltpu.VMEM((chunks, per * cells, LANES), jnp.float32),
            pltpu.VMEM((2, per, rays), jnp.float32),
            pltpu.VMEM((2, per, rays), jnp.float32),
            pltpu.VMEM((quarters, 4, per, width), jnp.float32),
            pltpu.VMEM((2, quarters, 4, per, width), jnp.float32),
            dma((chunks,)),
            dma((2,)),
            dma((2,)),
            dma((2, quarters)),
            dma((2, quarters)),
        ],
        compiler_params=pltpu.CompilerParams(collective_id=0, has_side_effects=True),
        name="front",
    )(patches.reshape(per * cells, rays))


def pack(tiles, slots, values_ref, row_ref, col_ref, out_ref, send):
    per = row_ref.shape[1]
    parts, _, _, width = out_ref.shape
    row, col = row_ref[...], col_ref[...]
    shift = per.bit_length() - 1
    dest_row, dest_col = row >> shift, col >> shift
    same = (dest_col == dest_row).astype(jnp.float32)
    down = lax.broadcasted_iota(jnp.int32, (per, per), 0)
    across = lax.broadcasted_iota(jnp.int32, (per, per), 1)
    rank_row = jnp.sum(jnp.where(down < across, same, 0.0), axis=0, keepdims=True)
    rank_col = jnp.sum(jnp.where(across < down, same, 0.0), axis=1, keepdims=True)
    target_row = dest_row * slots + rank_row.astype(jnp.int32)
    target_col = dest_col * slots + rank_col.astype(jnp.int32)
    offset = (col & (per - 1)).astype(jnp.float32) + 1.0
    choice = (
        lax.broadcasted_iota(jnp.int32, (tiles * slots, per), 0) == target_row
    ).astype(jnp.float32)
    lane = lax.broadcasted_iota(jnp.int32, (per, width), 1)
    for tile in range(tiles):
        hit = (target_col == tile * slots + lane) & (lane < slots)
        mark = jnp.sum(jnp.where(hit, offset, 0.0), axis=0, keepdims=True) - 1.0
        for half in range(parts):
            out_ref[half, tile, 4 * slots :, :] = jnp.broadcast_to(mark, (LABEL_ROWS, width))
    for half in range(parts):
        for c in range(4):
            packed = jnp.dot(
                choice,
                values_ref[c, :, half * width : (half + 1) * width],
                precision=lax.Precision.HIGHEST,
                preferred_element_type=jnp.float32,
            )
            out_ref[half, :, c * slots : (c + 1) * slots, :] = packed.reshape(
                tiles, slots, width
            )
        send(half)


def place(slots, got_ref, out_ref):
    tiles, width = got_ref.shape[0], got_ref.shape[2]
    quarters, _, share, _ = out_ref.shape
    per = quarters * share
    at = lax.broadcasted_iota(jnp.int32, (per, slots), 0)
    totals = [jnp.zeros((per, width), jnp.float32) for _ in range(4)]
    for tile in range(tiles):
        mark = got_ref[tile, 4 * slots : 4 * slots + 1, :][:, :slots].astype(jnp.int32)
        choice = (at == mark).astype(jnp.float32)
        for c in range(4):
            totals[c] = totals[c] + jnp.dot(
                choice,
                got_ref[tile, c * slots : (c + 1) * slots, :],
                precision=lax.Precision.HIGHEST,
                preferred_element_type=jnp.float32,
            )
    totals[3] = 1.0 - totals[3]
    for c in range(4):
        out_ref[:, c] = totals[c].reshape(quarters, share, width)


class Exchange:
    def __init__(self, axis, count, source_ref, got_ref, send_sem, recv_sem):
        self.axis, self.me = axis, lax.axis_index(axis)
        self.peers = [lax.rem(self.me + k, count) for k in range(1, count)]
        self.refs = source_ref, got_ref, send_sem, recv_sem

    def copy(self, half, piece, source, peer):
        source_ref, got_ref, send_sem, recv_sem = self.refs
        return pltpu.make_async_remote_copy(
            src_ref=source_ref.at[half, piece],
            dst_ref=got_ref.at[half, source],
            send_sem=send_sem.at[half, peer],
            recv_sem=recv_sem.at[half, source],
            device_id={self.axis: peer},
            device_id_type=MESH,
        )

    def start(self, half):
        source_ref, got_ref = self.refs[:2]
        for peer in self.peers:
            self.copy(half, peer, self.me, peer).start()
        got_ref[half, self.me] = source_ref[half, self.me]

    def arrive(self, half):
        for peer in self.peers:
            self.copy(half, self.me, peer, peer).wait_recv()

    def drain(self, half):
        for peer in self.peers:
            self.copy(half, peer, self.me, peer).wait_send()


def back_kernel(
    tiles, quarters, slots, values_ref, row_ref, col_ref, out_ref,
    packed, got, placed, landed, tile_send, tile_recv, depth_send, depth_recv,
):
    peers = [
        {axis: lax.rem(lax.axis_index(axis) + k, count)}
        for axis, count in (("tile", tiles), ("depth", quarters))
        for k in range(1, count)
    ]
    greet(peers)
    over_tile = Exchange("tile", tiles, packed, got, tile_send, tile_recv)
    over_depth = Exchange("depth", quarters, placed, landed, depth_send, depth_recv)
    pack(tiles, slots, values_ref, row_ref, col_ref, packed, over_tile.start)
    halves = range(packed.shape[0])
    width = packed.shape[3]
    for half in halves:
        over_tile.arrive(half)
        place(slots, got.at[half], placed.at[half])
        over_depth.start(half)
    for half in halves:
        over_depth.arrive(half)
        out_ref[:, :, :, half * width : (half + 1) * width] = landed[half]
    for half in halves:
        over_tile.drain(half)
        over_depth.drain(half)


def back(values, patch_slot, tiles, quarters, slots):
    _, per, width = values.shape
    dma = pltpu.SemaphoreType.DMA
    result = (quarters, 4, per // quarters, width)
    halves = width // LANES
    piece = (halves, quarters, 4, per // quarters, LANES)
    block = (halves, tiles, 4 * slots + LABEL_ROWS, LANES)
    return pl.pallas_call(
        functools.partial(back_kernel, tiles, quarters, slots),
        out_shape=jax.ShapeDtypeStruct(result, jnp.float32),
        in_specs=[pl.BlockSpec(memory_space=pltpu.VMEM)] * 3,
        out_specs=pl.BlockSpec(memory_space=pltpu.VMEM),
        scratch_shapes=[
            pltpu.VMEM(block, jnp.float32),
            pltpu.VMEM(block, jnp.float32),
            pltpu.VMEM(piece, jnp.float32),
            pltpu.VMEM(piece, jnp.float32),
            dma((halves, tiles)),
            dma((halves, tiles)),
            dma((halves, quarters)),
            dma((halves, quarters)),
        ],
        compiler_params=pltpu.CompilerParams(collective_id=1, has_side_effects=True),
        name="back",
    )(values, patch_slot.reshape(1, per), patch_slot.reshape(per, 1))


def local(patches, patch_slot):
    per, _, rays = patches.shape
    tiles = lax.axis_size("tile")
    quarters = lax.axis_size("depth")
    slots = -(-(3 * per // tiles) // 8) * 8
    values = front(patches, quarters)
    final = back(values, patch_slot, tiles, quarters, slots)
    return final.transpose(2, 1, 0, 3).reshape(1, per // quarters, 4, rays)


def solution(mesh):
    return jax.shard_map(
        local,
        mesh=mesh,
        in_specs=(P("tile", "depth", None), P("tile")),
        out_specs=P("tile", "depth", None, None),
        check_vma=False,
    )
```

```python
import functools
import math

import jax
import jax.numpy as jnp
from jax import lax
from jax.experimental import pallas as pl
from jax.experimental.pallas import tpu as pltpu
from jax.sharding import PartitionSpec as P

BLOCK = 8
GROUPS = 2
LANES = 128
MESH = pl.DeviceIdType.MESH
LABEL_ROWS = 8


def ray_cell(scale, state, x, before, level, after):
    red, green, blue, clear = state
    slope = (after - before) * 0.5
    slope2 = slope * slope
    square = x * x
    bell = jnp.exp(-level * level)
    wide = 1.0 + square
    below = wide * (1.0 + slope2)
    inverse = 1.0 / (square * below)
    ratio = bell * (inverse * below)
    optical = (
        (0.6 * math.exp(-0.25) * scale) * (bell * x)
        + (0.4 * math.exp(-2.0) * scale) * (ratio * ratio)
        + (0.3 * scale) * slope2
    )
    pass_on = jnp.exp(-optical)
    light = clear * (1.0 - pass_on) * (inverse * square)
    return (
        red + light * square,
        green + light * (bell * wide),
        blue + light,
        clear * pass_on,
    )


def over(front, back):
    clear = front[3]
    return tuple(front[c] + clear * back[c] for c in range(3)) + (clear * back[3],)


def greet(peers):
    barrier = pltpu.get_barrier_semaphore()
    for peer in peers:
        pl.semaphore_signal(barrier, inc=1, device_id=peer, device_id_type=MESH)
    pl.semaphore_wait(barrier, len(peers))


def front_kernel(
    cells, quarters, scale, x_hbm, out_ref,
    x_ref, edge, halo, part, got, load_sem, edge_send, edge_recv, send_sem, recv_sem,
):
    me = lax.axis_index("depth")
    _, per, width = out_ref.shape
    halves = width // LANES
    chunks = quarters * halves
    rows = GROUPS * BLOCK
    shape = (GROUPS, BLOCK, LANES)
    loads = [
        pltpu.make_async_copy(
            x_hbm.at[:, pl.ds(j * LANES, LANES)], x_ref.at[j], load_sem.at[j]
        )
        for j in range(chunks)
    ]
    for load in loads:
        load.start()
    greet([{"depth": lax.rem(me + k, quarters)} for k in range(1, quarters)])

    def plane(chunk, step, cell):
        base = step * (rows * cells) + cell
        return jnp.stack(
            [
                x_ref[chunk, pl.ds(base + g * BLOCK * cells, BLOCK, stride=cells), :]
                for g in range(GROUPS)
            ]
        )

    def patch_rows(step):
        return pl.ds(pl.multiple_of(step * rows, rows), rows)

    for j in range(chunks):
        loads[j].wait()

        @pl.loop(0, per // rows)
        def _(step):
            for side, cell in enumerate((0, cells - 1)):
                value = jnp.log(plane(j, step, cell)).reshape(rows, LANES)
                edge[side, patch_rows(step), pl.ds(j * LANES, LANES)] = value

    def edge_copy(side, source, peer):
        return pltpu.make_async_remote_copy(
            src_ref=edge.at[source],
            dst_ref=halo.at[side],
            send_sem=edge_send.at[side],
            recv_sem=edge_recv.at[side],
            device_id={"depth": peer},
            device_id_type=MESH,
        )

    up = edge_copy(0, 1, lax.rem(me + 1, quarters))
    down = edge_copy(1, 0, lax.rem(me + quarters - 1, quarters))

    @pl.when(me < quarters - 1)
    def _():
        up.start()

    @pl.when(me > 0)
    def _():
        down.start()

    @pl.when(me == 0)
    def _():
        halo[0] = jnp.zeros_like(halo[0])

    @pl.when(me == quarters - 1)
    def _():
        halo[1] = jnp.zeros_like(halo[1])

    ones = functools.partial(jnp.ones, shape, jnp.float32)
    zeros = functools.partial(jnp.zeros, shape, jnp.float32)

    def interior(quarter, half):
        chunk = quarter * halves + half
        lanes = pl.ds(half * LANES, LANES)

        @pl.loop(0, per // rows)
        def _(step):
            before = jnp.log(plane(chunk, step, 0))
            x = plane(chunk, step, 1)
            level = jnp.log(x)
            state = (zeros(), zeros(), zeros(), ones())
            for cell in range(1, cells - 1):
                x_after = plane(chunk, step, cell + 1)
                after = jnp.log(x_after)
                state = ray_cell(scale, state, x, before, level, after)
                before, level, x = level, after, x_after
            for c in range(4):
                part[quarter, c, patch_rows(step), lanes] = state[c].reshape(rows, LANES)

    last = quarters - 1
    near = (me < quarters // 2).astype(jnp.int32)
    order = [k + near * (last - 2 * k) for k in range(quarters)]
    for quarter in order[:last]:
        for half in range(halves):
            interior(quarter, half)

    @pl.when(me > 0)
    def _():
        up.wait_recv()

    @pl.when(me < quarters - 1)
    def _():
        down.wait_recv()

    def hop(side, quarter):
        peer = lax.rem(me + (quarters - 1 if side else 1), quarters)
        return pltpu.make_async_remote_copy(
            src_ref=part.at[quarter],
            dst_ref=got.at[side, quarter],
            send_sem=send_sem.at[side, quarter],
            recv_sem=recv_sem.at[side, quarter],
            device_id={"depth": peer},
            device_id_type=MESH,
        )

    def finish(quarter):
        for half in range(halves):
            chunk = quarter * halves + half
            lanes = pl.ds(half * LANES, LANES)
            wide = pl.ds(pl.multiple_of(chunk * LANES, LANES), LANES)

            @pl.loop(0, per // rows)
            def _(step):
                start = (zeros(), zeros(), zeros(), ones())
                x = plane(chunk, step, 0)
                first = ray_cell(
                    scale, start, x,
                    halo[0, patch_rows(step), wide].reshape(shape),
                    jnp.log(x),
                    jnp.log(plane(chunk, step, 1)),
                )
                x = plane(chunk, step, cells - 1)
                last = ray_cell(
                    scale, start, x,
                    jnp.log(plane(chunk, step, cells - 2)),
                    jnp.log(x),
                    halo[1, patch_rows(step), wide].reshape(shape),
                )
                inner = tuple(
                    part[quarter, c, patch_rows(step), lanes].reshape(shape)
                    for c in range(4)
                )
                total = over(over(first, inner), last)
                for c in range(4):
                    part[quarter, c, patch_rows(step), lanes] = total[c].reshape(rows, LANES)

    for k, quarter in enumerate(order):
        if k == last:
            for half in range(halves):
                interior(quarter, half)
        finish(quarter)
        if k < last:
            for side, end in enumerate((0, last)):
                @pl.when(me == end)
                def _():
                    hop(side, last - k if side == 0 else k).start()

    def merge(side, quarter):
        own = tuple(part[quarter, c] for c in range(4))
        come = tuple(got[side, quarter, c] for c in range(4))
        total = over(own, come) if side else over(come, own)
        for c in range(4):
            part[quarter, c] = total[c]

    def turn(side, t):
        rank = last - me if side else me
        quarter = t - rank if side else last - t + rank
        return rank, quarter

    for t in range(1, last):
        for side in (0, 1):
            rank, quarter = turn(side, t)

            @pl.when((rank >= 1) & (rank <= t))
            def _():
                hop(side, quarter).wait_recv()
                merge(side, quarter)
                hop(side, quarter).start()

    for side, end in enumerate((0, last)):
        @pl.when(me != end)
        def _():
            hop(side, me).wait_recv()
            merge(side, me)

    for c in range(4):
        out_ref[c] = part[me, c]
    for t in range(last):
        for side in (0, 1):
            rank, quarter = turn(side, t)

            @pl.when(rank <= t)
            def _():
                hop(side, quarter).wait_send()

    @pl.when(me < quarters - 1)
    def _():
        up.wait_send()

    @pl.when(me > 0)
    def _():
        down.wait_send()


def front(patches, quarters):
    per, cells, rays = patches.shape
    width = rays // quarters
    chunks = rays // LANES
    dma = pltpu.SemaphoreType.DMA
    return pl.pallas_call(
        functools.partial(front_kernel, cells, quarters, 2.0 / (cells * quarters)),
        out_shape=jax.ShapeDtypeStruct((4, per, width), jnp.float32),
        in_specs=[pl.BlockSpec(memory_space=pl.ANY)],
        out_specs=pl.BlockSpec(memory_space=pltpu.VMEM),
        scratch_shapes=[
            pltpu.VMEM((chunks, per * cells, LANES), jnp.float32),
            pltpu.VMEM((2, per, rays), jnp.float32),
            pltpu.VMEM((2, per, rays), jnp.float32),
            pltpu.VMEM((quarters, 4, per, width), jnp.float32),
            pltpu.VMEM((2, quarters, 4, per, width), jnp.float32),
            dma((chunks,)),
            dma((2,)),
            dma((2,)),
            dma((2, quarters)),
            dma((2, quarters)),
        ],
        compiler_params=pltpu.CompilerParams(collective_id=0, has_side_effects=True),
        name="front",
    )(patches.reshape(per * cells, rays))


def pack(tiles, slots, values_ref, row_ref, out_ref, send):
    per = row_ref.shape[1]
    parts, _, _, width = out_ref.shape
    row = row_ref[...]
    down = lax.broadcasted_iota(jnp.int32, (per, per), 0)
    across = lax.broadcasted_iota(jnp.int32, (per, per), 1)
    col = jnp.sum(
        jnp.where(down == across, row.astype(jnp.float32), 0.0), axis=1, keepdims=True
    ).astype(jnp.int32)
    shift = per.bit_length() - 1
    dest_row, dest_col = row >> shift, col >> shift
    same = (dest_col == dest_row).astype(jnp.float32)
    rank_row = jnp.sum(jnp.where(down < across, same, 0.0), axis=0, keepdims=True)
    rank_col = jnp.sum(jnp.where(across < down, same, 0.0), axis=1, keepdims=True)
    target_row = dest_row * slots + rank_row.astype(jnp.int32)
    target_col = dest_col * slots + rank_col.astype(jnp.int32)
    offset = (col & (per - 1)).astype(jnp.float32) + 1.0
    choice = (
        lax.broadcasted_iota(jnp.int32, (tiles * slots, per), 0) == target_row
    ).astype(jnp.float32)
    lane = lax.broadcasted_iota(jnp.int32, (per, width), 1)
    for tile in range(tiles):
        hit = (target_col == tile * slots + lane) & (lane < slots)
        mark = jnp.sum(jnp.where(hit, offset, 0.0), axis=0, keepdims=True) - 1.0
        for half in range(parts):
            out_ref[half, tile, 4 * slots :, :] = jnp.broadcast_to(mark, (LABEL_ROWS, width))
    for half in range(parts):
        for c in range(4):
            packed = jnp.dot(
                choice,
                values_ref[c, :, half * width : (half + 1) * width],
                precision=lax.Precision.HIGHEST,
                preferred_element_type=jnp.float32,
            )
            out_ref[half, :, c * slots : (c + 1) * slots, :] = packed.reshape(
                tiles, slots, width
            )
        send(half)


def place(slots, got_ref, out_ref):
    tiles, width = got_ref.shape[0], got_ref.shape[2]
    quarters, _, share, _ = out_ref.shape
    per = quarters * share
    at = lax.broadcasted_iota(jnp.int32, (per, slots), 0)
    totals = [jnp.zeros((per, width), jnp.float32) for _ in range(4)]
    for tile in range(tiles):
        mark = got_ref[tile, 4 * slots : 4 * slots + 1, :][:, :slots].astype(jnp.int32)
        choice = (at == mark).astype(jnp.float32)
        for c in range(4):
            totals[c] = totals[c] + jnp.dot(
                choice,
                got_ref[tile, c * slots : (c + 1) * slots, :],
                precision=lax.Precision.HIGHEST,
                preferred_element_type=jnp.float32,
            )
    totals[3] = 1.0 - totals[3]
    for c in range(4):
        out_ref[:, c] = totals[c].reshape(quarters, share, width)


class Exchange:
    def __init__(self, axis, count, source_ref, got_ref, send_sem, recv_sem):
        self.axis, self.me = axis, lax.axis_index(axis)
        self.peers = [lax.rem(self.me + k, count) for k in range(1, count)]
        self.refs = source_ref, got_ref, send_sem, recv_sem

    def copy(self, half, piece, source, peer):
        source_ref, got_ref, send_sem, recv_sem = self.refs
        return pltpu.make_async_remote_copy(
            src_ref=source_ref.at[half, piece],
            dst_ref=got_ref.at[half, source],
            send_sem=send_sem.at[half, peer],
            recv_sem=recv_sem.at[half, source],
            device_id={self.axis: peer},
            device_id_type=MESH,
        )

    def start(self, half):
        source_ref, got_ref = self.refs[:2]
        for peer in self.peers:
            self.copy(half, peer, self.me, peer).start()
        got_ref[half, self.me] = source_ref[half, self.me]

    def arrive(self, half):
        for peer in self.peers:
            self.copy(half, self.me, peer, peer).wait_recv()

    def drain(self, half):
        for peer in self.peers:
            self.copy(half, peer, self.me, peer).wait_send()


def back_kernel(
    tiles, quarters, slots, values_ref, row_ref, out_ref,
    packed, got, placed, landed, tile_send, tile_recv, depth_send, depth_recv,
):
    peers = [
        {axis: lax.rem(lax.axis_index(axis) + k, count)}
        for axis, count in (("tile", tiles), ("depth", quarters))
        for k in range(1, count)
    ]
    greet(peers)
    over_tile = Exchange("tile", tiles, packed, got, tile_send, tile_recv)
    over_depth = Exchange("depth", quarters, placed, landed, depth_send, depth_recv)
    pack(tiles, slots, values_ref, row_ref, packed, over_tile.start)
    halves = range(packed.shape[0])
    width = packed.shape[3]
    for half in halves:
        over_tile.arrive(half)
        place(slots, got.at[half], placed.at[half])
        over_depth.start(half)
    for half in halves:
        over_depth.arrive(half)
        for quarter in range(quarters):
            start = (quarter * len(halves) + half) * width
            for c in range(4):
                out_ref[:, c, start : start + width] = landed[half, quarter, c]
    for half in halves:
        over_tile.drain(half)
        over_depth.drain(half)


def back(values, patch_slot, tiles, quarters, slots):
    _, per, width = values.shape
    dma = pltpu.SemaphoreType.DMA
    result = (per // quarters, 4, quarters * width)
    halves = width // LANES
    piece = (halves, quarters, 4, per // quarters, LANES)
    block = (halves, tiles, 4 * slots + LABEL_ROWS, LANES)
    return pl.pallas_call(
        functools.partial(back_kernel, tiles, quarters, slots),
        out_shape=jax.ShapeDtypeStruct(result, jnp.float32),
        in_specs=[pl.BlockSpec(memory_space=pltpu.VMEM)] * 2,
        out_specs=pl.BlockSpec(memory_space=pltpu.VMEM),
        scratch_shapes=[
            pltpu.VMEM(block, jnp.float32),
            pltpu.VMEM(block, jnp.float32),
            pltpu.VMEM(piece, jnp.float32),
            pltpu.VMEM(piece, jnp.float32),
            dma((halves, tiles)),
            dma((halves, tiles)),
            dma((halves, quarters)),
            dma((halves, quarters)),
        ],
        compiler_params=pltpu.CompilerParams(collective_id=1, has_side_effects=True),
        name="back",
    )(values, patch_slot.reshape(1, per))


def local(patches, patch_slot):
    per = patches.shape[0]
    tiles = lax.axis_size("tile")
    quarters = lax.axis_size("depth")
    slots = -(-(3 * per // tiles) // 8) * 8
    values = front(patches, quarters)
    final = back(values, patch_slot, tiles, quarters, slots)
    return final.reshape((1,) + final.shape)


def solution(mesh):
    return jax.shard_map(
        local,
        mesh=mesh,
        in_specs=(P("tile", "depth", None), P("tile")),
        out_specs=P("tile", "depth", None, None),
        check_vma=False,
    )
```
